256 devices in a mesh: col: 128 (over x, y_hi, z, core), band: 2 (over y_lo).
Axes of the slice: x: 4, y: 4 (y_hi: 2, y_lo: 2; y = y_hi * 2 + y_lo), z: 8, core: 2. Of those that a mesh axis runs over, the one named last changes fastest.
Arguments:
- boundary: bfloat16 [128, 3, 128, 16, 128], P('col'), may hold values from -6 to 6
- row_tensor: bfloat16 [2, 128, 16, 16, 16, 16], P('band', 'col'), may hold values from -1.5 to 1.5
- right_proj: bfloat16 [2, 128, 3, 128, 16, 128], P('band', 'col'), may hold values from -0.125 to 0.125
- left_proj: bfloat16 [2, 128, 3, 128, 16, 128], P('band', 'col'), may hold values from -0.125 to 0.125
- kept: int32 [2, 128, 3], P('band', 'col'), may hold values from 64 to 128, as said below
Outputs:
- evolved: bfloat16 [2, 128, 3, 128, 16, 128], P('band', 'col')
The draws below stay inside these ranges and needn't reach their ends.
Inputs may be any that keep to these rules, and one draw needn't show every extreme that they name: kept[r, c, s] counts the live states of sector s on the bond between columns c and (c + 1) mod 128; the value 128 occurs in every draw.
All inputs are finite; a program needn't handle non-finite values.
Results may differ from the reference program's by a relative error of at most 0.0095.
Values may be sent and summed in bfloat16 or wider, within the bound.
No kernel may reach another device: no remote copies, remote signals or barrier semaphores. Data moves between devices by JAX's collectives and lax.ppermute only.
A program may use at most 64 MiB of HBM per device.

```python
import jax
import jax.numpy as jnp
from jax import lax

W = 128
SECT = 3
D2 = 16
COLS = 128
ROWS = 2


def draw_kept(key, part):
    first_key, second_key = jax.random.split(key)
    values = jax.random.randint(first_key, (ROWS, COLS, SECT), W // 2, W + 1)
    chosen = jax.random.randint(second_key, (), 0, ROWS * COLS * SECT)
    places = jnp.arange(ROWS * COLS * SECT).reshape(ROWS, COLS, SECT)
    return jnp.where(places == chosen, W, values).astype(jnp.int32)


def steps_of(stream_key, dims, cuts, low, high):
    factor_of, own = 1.0, jax.random.fold_in(stream_key, 6)
    for dim, parts in cuts:
        steps = jnp.exp(jax.random.uniform(jax.random.fold_in(own, dim), (parts,), jnp.float32, low / len(cuts), high / len(cuts)))
        factor_of = factor_of * jnp.repeat(steps, dims[dim] // parts).reshape([-1 if axis == dim else 1 for axis in range(len(dims))])
    return factor_of


def scatter_about(key, dims, spread, reach, cuts=(), dtype=jnp.bfloat16):
    factor_of = steps_of(key, dims, cuts, -0.22, 0.18) if cuts else 1.0
    array = jax.random.normal(key, dims, jnp.float32) * spread * factor_of
    return jnp.minimum(jnp.maximum(array, -reach), reach).astype(dtype)


def setup_inputs(seed: int = 0) -> dict:
    key_of = jax.random.split(jax.random.key(seed), 6)
    boundary = scatter_about(key_of[0], (COLS, SECT, W, D2, W), 1.0, 6.0, ((0, 128),))
    row_tensor = scatter_about(key_of[1], (ROWS, COLS, D2, D2, D2, D2), D2 ** -0.5, 1.5, ((0, 2), (1, 128)))
    right_proj = scatter_about(key_of[2], (ROWS, COLS, SECT, W, D2, W), (W * D2) ** -0.5, 0.125, ((0, 2), (1, 128)))
    left_proj = scatter_about(key_of[3], (ROWS, COLS, SECT, W, D2, W), (W * D2) ** -0.5, 0.125, ((0, 2), (1, 128)))
    kept = draw_kept(jax.random.fold_in(key_of[5], 71), 0)
    return {"boundary": boundary, "row_tensor": row_tensor, "right_proj": right_proj, "left_proj": left_proj, "kept": kept}


def sector_update(sector_block, layer_tensor, right_half, left_half, keep_left, keep_right):
    halfway = jnp.einsum('apb,btc->aptc', sector_block.astype(jnp.float32), right_half.astype(jnp.float32)).astype(jnp.bfloat16)
    halfway = lax.optimization_barrier(halfway)
    widened = jnp.einsum('aptc,lpqt->alqc', halfway.astype(jnp.float32), layer_tensor.astype(jnp.float32)).astype(jnp.bfloat16)
    widened = lax.optimization_barrier(widened)
    updated = jnp.einsum('alf,alqc->fqc', left_half.astype(jnp.float32), widened.astype(jnp.float32))
    left_range = jnp.arange(updated.shape[0])
    right_range = jnp.arange(updated.shape[2])
    kept_mask = (left_range < keep_left)[:, None, None] & (right_range < keep_right)[None, None, :]
    return jnp.where(kept_mask, updated, jnp.float32(0.0)).astype(jnp.bfloat16)


def column_update(column_state, layer_tensor, right_half, left_half, keep_left, keep_right):
    def per_sector(position):
        return sector_update(column_state[position], layer_tensor, right_half[position], left_half[position], keep_left[position], keep_right[position])
    return lax.map(per_sector, jnp.arange(column_state.shape[0]))


def reference(boundary, row_tensor, right_proj, left_proj, kept):
    boundary_state = boundary
    results = []
    for row_index in range(ROWS):
        shifted_left = jnp.roll(left_proj[row_index], 1, axis=0)
        left_kept = jnp.roll(kept[row_index], 1, axis=0)
        current = boundary_state

        def per_column(column):
            return column_update(current[column], row_tensor[row_index, column], right_proj[row_index, column], shifted_left[column], left_kept[column], kept[row_index, column])

        boundary_state = lax.map(per_column, jnp.arange(COLS))
        results.append(boundary_state)
    return jnp.stack(results)
```

```python
import functools

import jax
import jax.numpy as jnp
from jax import lax
from jax.experimental import pallas as pl
from jax.experimental.pallas import tpu as pltpu
from jax.sharding import PartitionSpec as P

F32, BF16 = jnp.float32, jnp.bfloat16
ANY = pl.BlockSpec(memory_space=pl.ANY)
SMEM = pl.BlockSpec(memory_space=pltpu.SMEM)
VMEM_LIMIT = 48 << 20


def shift_pairs(n):
    return [((i - 1) % n, i) for i in range(n)]


def contract_right(x, rp, rp32, h):
    W, D, _ = x.shape
    rp32[...] = rp[...].reshape(W * D, W).astype(F32)
    rows = x[...].reshape(W * D, W)
    for t in range(0, D, 2):
        pair = [rp32[pl.ds(t + i, W, stride=D), :].astype(BF16) for i in range(2)]
        y = jnp.dot(rows, jnp.concatenate(pair, axis=1), preferred_element_type=F32).astype(BF16)
        h[t] = y[:, :W].reshape(W, D, W)
        h[t + 1] = y[:, W:].reshape(W, D, W)


def contract_layer(r, h, w):
    D, W = h.shape[0], h.shape[1]
    layer = r[...]

    def step(i, _):
        a = 2 * i
        pair = [h[:, a + k].reshape(D * D, W) for k in range(2)]
        y = jnp.dot(layer, jnp.concatenate(pair, axis=1), preferred_element_type=F32).astype(BF16)
        for k in range(2):
            w[:, a + k] = y[:, k * W : (k + 1) * W].reshape(D, D, W)
        return 0

    lax.fori_loop(0, W // 2, step, 0, unroll=32)


def flip_left(lp, lpt):
    W, D, _ = lp.shape
    lpt[...] = lp[...].reshape(W * D, W).T


def contract_left(lpt, w, keep_left, keep_right, out32, out, ready=None):
    D, W = w.shape[0], w.shape[1]
    left = lpt[...]
    rows = lax.broadcasted_iota(jnp.int32, (W, W), 0)
    lanes = lax.broadcasted_iota(jnp.int32, (W, W), 1)
    live = (rows < keep_left) & (lanes < keep_right)
    for q in range(0, D, 2):
        if ready is not None:
            ready(q)
        pair = [w[q + k].reshape(W * D, W) for k in range(2)]
        y = jnp.dot(left, jnp.concatenate(pair, axis=1), preferred_element_type=F32)
        for k in range(2):
            out32[pl.ds(q + k, W, stride=D), :] = jnp.where(live, y[:, k * W : (k + 1) * W], 0.0)
    out[...] = out32[...].astype(BF16).reshape(out.shape)


def scratch(W, D):
    big = pltpu.VMEM((D, W, D, W), BF16)
    block = pltpu.VMEM((W, D, W), BF16)
    return dict(
        x=block, rp=block, lp=block, r=pltpu.VMEM((D * D, D * D), BF16),
        rp32=pltpu.VMEM((W * D, W), F32), h=big, w=big,
        lpt=pltpu.VMEM((W, W * D), BF16), out32=pltpu.VMEM((W * D, W), F32), out=block,
    )


def load(src, dst, sem):
    copy = pltpu.make_async_copy(src, dst, sem)
    copy.start()
    return copy


def head_kernel(s, band, meta, boundary, right, layer, w_hbm, x, rp, r, rp32, h, w, sems):
    @pl.when(meta[0] == band)
    def _():
        copies = [
            load(right.at[0, 0, s], rp, sems.at[0]),
            load(boundary.at[0, s], x, sems.at[1]),
            load(layer, r, sems.at[2]),
        ]
        for copy in copies:
            copy.wait()
        contract_right(x, rp, rp32, h)
        contract_layer(r, h, w)
        pltpu.sync_copy(w, w_hbm)


def tail_kernel(s, band, sectors, meta, left, w_hbm, state, lp, w, lpt, out32, out, sems):
    @pl.when(meta[0] == band)
    def _():
        D = w.shape[0]
        first = load(left, lp, sems.at[0])
        parts = [load(w_hbm.at[pl.ds(q, 2)], w.at[pl.ds(q, 2)], sems.at[1 + q // 2]) for q in range(0, D, 2)]
        first.wait()
        flip_left(lp, lpt)
        contract_left(
            lpt, w, meta[1 + sectors + s], meta[1 + s], out32, out, lambda q: parts[q // 2].wait()
        )
        pltpu.sync_copy(out, state)


def full_sector(s, sectors, meta, state_in, right, layer, left, target, x, rp, lp, r, rp32, h, w, lpt, out32, out, sems):
    copies = [
        load(right.at[0, 0, s], rp, sems.at[0]),
        load(state_in, x, sems.at[1]),
        load(layer, r, sems.at[2]),
        load(left, lp, sems.at[3]),
    ]
    for copy in copies:
        copy.wait()
    contract_right(x, rp, rp32, h)
    contract_layer(r, h, w)
    flip_left(lp, lpt)
    contract_left(lpt, w, meta[1 + sectors + s], meta[1 + s], out32, out)
    pltpu.sync_copy(out, target)


def upper_kernel(s, sectors, meta, boundary, right, layer, left, state, *rest):
    @pl.when(meta[0] == 0)
    def _():
        full_sector(s, sectors, meta, boundary.at[0, s], right, layer, left, state, *rest)


def lower_kernel(s, sectors, aliased, meta, *refs):
    if aliased:
        refs = refs[1:]
    own, arrived, right, layer, left, result, *rest = refs
    target = result.at[0, 0, s]

    @pl.when(meta[0] == 0)
    def _():
        pltpu.sync_copy(own, target)

    @pl.when(meta[0] == 1)
    def _():
        full_sector(s, sectors, meta, arrived, right, layer, left, target, *rest)


def body(boundary, row_tensor, right_proj, left_proj, kept):
    _, sectors, W, D, _ = boundary.shape
    band = lax.axis_index("band")
    cols = shift_pairs(lax.axis_size("col"))
    down = [(0, 1)]
    keep_left = lax.ppermute(kept[0, 0], "col", cols)
    left = [lax.ppermute(left_proj[0, 0, s], "col", cols) for s in range(sectors)]
    meta = jnp.concatenate([band[None].astype(jnp.int32), kept[0, 0], keep_left])
    layer = row_tensor[0, 0].transpose(2, 0, 3, 1).reshape(D * D, D * D)

    sc = scratch(W, D)
    block = jax.ShapeDtypeStruct((W, D, W), BF16)
    dma = pltpu.SemaphoreType.DMA((9,))
    params = pltpu.CompilerParams(vmem_limit_bytes=VMEM_LIMIT)

    def cost(part):
        flops = int(8 * part * W * D * W * W * D)
        return pl.CostEstimate(flops=flops, bytes_accessed=4 * 2 * W * D * W, transcendentals=0)

    wide = pl.pallas_call(
        functools.partial(head_kernel, 0, 0),
        out_shape=jax.ShapeDtypeStruct((D, W, D, W), BF16),
        in_specs=[SMEM, ANY, ANY, ANY], out_specs=ANY,
        scratch_shapes=[sc[k] for k in ("x", "rp", "r", "rp32", "h", "w")] + [dma],
        compiler_params=params, cost_estimate=cost(0.75), name="head",
    )(jnp.stack([band.astype(jnp.int32)]), boundary, right_proj, layer)
    state = [
        pl.pallas_call(
            functools.partial(tail_kernel, 0, 0, sectors),
            out_shape=block, in_specs=[SMEM, ANY, ANY], out_specs=ANY,
            scratch_shapes=[sc[k] for k in ("lp", "w", "lpt", "out32", "out")] + [dma],
            compiler_params=params, cost_estimate=cost(0.25), name="tail",
        )(meta, left[0], wide)
    ]
    names = ("x", "rp", "lp", "r", "rp32", "h", "w", "lpt", "out32", "out")
    arrived = [lax.ppermute(state[0], "band", down)]
    for s in range(1, sectors):
        state.append(
            pl.pallas_call(
                functools.partial(upper_kernel, s, sectors),
                out_shape=block, in_specs=[SMEM, ANY, ANY, ANY, ANY], out_specs=ANY,
                scratch_shapes=[sc[k] for k in names] + [dma],
                compiler_params=params, cost_estimate=cost(1), name="upper",
            )(meta, boundary, right_proj, layer, left[s])
        )
        arrived.append(lax.ppermute(state[s], "band", down))
    result = None
    for s in range(sectors):
        head = [] if result is None else [result]
        result = pl.pallas_call(
            functools.partial(lower_kernel, s, sectors, bool(head)),
            out_shape=jax.ShapeDtypeStruct((1, 1, sectors, W, D, W), BF16),
            in_specs=[SMEM] + [ANY] * (5 + len(head)), out_specs=ANY,
            scratch_shapes=[sc[k] for k in names] + [dma],
            input_output_aliases={1: 0} if head else {},
            compiler_params=params, cost_estimate=cost(1), name="lower",
        )(meta, *head, state[s], arrived[s], right_proj, layer, left[s])
    return result


def solution(mesh):
    in_specs = (
        P("col", None, None, None, None),
        P("band", "col", None, None, None, None),
        P("band", "col", None, None, None, None),
        P("band", "col", None, None, None, None),
        P("band", "col", None),
    )
    out_specs = P("band", "col", None, None, None, None)
    return jax.shard_map(body, mesh=mesh, in_specs=in_specs, out_specs=out_specs, check_vma=False)
```

```python
import functools

import jax
import jax.numpy as jnp
from jax import lax
from jax.experimental import pallas as pl
from jax.experimental.pallas import tpu as pltpu
from jax.sharding import PartitionSpec as P

F32, BF16 = jnp.float32, jnp.bfloat16
ANY = pl.BlockSpec(memory_space=pl.ANY)
HBM = pl.BlockSpec(memory_space=pltpu.HBM)
SMEM = pl.BlockSpec(memory_space=pltpu.SMEM)
VMEM = pl.BlockSpec(memory_space=pltpu.VMEM)
PARAMS = pltpu.CompilerParams(vmem_limit_bytes=32 << 20)


def shift_pairs(n):
    return [((i - 1) % n, i) for i in range(n)]


def in_vmem(array):
    return pltpu.with_memory_space_constraint(array, pltpu.VMEM)


def in_hbm(array):
    return pltpu.with_memory_space_constraint(array, pltpu.HBM)


def contract_right(x, rp, rp32, h, at=0):
    n, D, W = x.shape
    rp32[...] = rp[...].reshape(W * D, W).astype(F32)
    rows = x[...].reshape(n * D, W)
    for t in range(0, D, 2):
        pair = [rp32[pl.ds(t + i, W, stride=D), :].astype(BF16) for i in range(2)]
        y = jnp.dot(rows, jnp.concatenate(pair, axis=1), preferred_element_type=F32).astype(BF16)
        h[t, at : at + n] = y[:, :W].reshape(n, D, W)
        h[t + 1, at : at + n] = y[:, W:].reshape(n, D, W)


def contract_layer(r, h, w, at=0, n=None):
    D, W = h.shape[0], h.shape[-1]
    n = h.shape[1] if n is None else n
    layer = r[...]

    def step(i, _):
        a = at + 2 * i
        pair = [h[:, a + k].reshape(D * D, W) for k in range(2)]
        y = jnp.dot(layer, jnp.concatenate(pair, axis=1), preferred_element_type=F32).astype(BF16)
        for k in range(2):
            w[:, a + k] = y[:, k * W : (k + 1) * W].reshape(D, D, W)
        return 0

    lax.fori_loop(0, n // 2, step, 0, unroll=32)


def flip_left(lp, lpt):
    D, W = lp.shape[1:]
    lpt[...] = lp[:W].reshape(W * D, W).T


def live_mask(lp, keep_right):
    W = lp.shape[-1]
    keep_left = lp[W, 0:1, :].astype(F32)
    rows = lax.broadcasted_iota(jnp.int32, (W, W), 0).astype(F32)
    lanes = lax.broadcasted_iota(jnp.int32, (W, W), 1)
    return (rows < keep_left) & (lanes < keep_right)


def contract_left(lpt, w, acc, at=0, n=None, carried=None, live=None):
    D, W = w.shape[0], w.shape[-1]
    n = w.shape[1] if n is None else n
    left = lpt[:, at * D : (at + n) * D]
    for q in range(0, D, 2):
        pair = [w[q + k, at : at + n].reshape(n * D, W) for k in range(2)]
        y = jnp.dot(left, jnp.concatenate(pair, axis=1), preferred_element_type=F32)
        for k in range(2):
            rows = pl.ds(q + k, W, stride=D)
            z = y[:, k * W : (k + 1) * W]
            if carried is not None:
                z = z + carried[rows, :]
            if live is not None:
                z = jnp.where(live, z, 0.0)
            acc[rows, :] = z


def store(acc, outs):
    at = 0
    for out in outs:
        n, D, W = out.shape
        out[...] = acc[at * D : (at + n) * D, :].astype(BF16).reshape(out.shape)
        at += n


def spread_layer(raw, r32, r):
    D = raw.shape[0]
    rows = lax.broadcasted_iota(jnp.int32, (D, D * D), 0)
    lanes = lax.broadcasted_iota(jnp.int32, (D, D * D), 1)
    total = jnp.zeros((D * D, D * D), F32)
    for p in range(D):
        place = (lanes == rows * D + p).astype(BF16)
        total += jnp.dot(raw[:, p].reshape(D * D, D), place, preferred_element_type=F32)
    n, W = D * D, r32.shape[1]
    for i in range(n // W):
        r32[i * n : (i + 1) * n, :] = total[:, i * W : (i + 1) * W]
        for q in range(D):
            r[q * D : (q + 1) * D, i * W : (i + 1) * W] = r32[pl.ds(i * n + q, D, stride=D), :].astype(BF16)


def load(src, dst, sem):
    copy = pltpu.make_async_copy(src, dst, sem)
    copy.start()
    return copy


def send_block(kept, s, left_proj, out, sem):
    W = left_proj.shape[3]
    copy = load(left_proj.at[0, 0, s], out.at[pl.ds(0, W)], sem)
    out[W] = jnp.full(out.shape[1:], kept[0, 0, s].astype(F32), F32).astype(BF16)
    return copy


def first_kernel(kept, left_proj, out, sems):
    send_block(kept, 0, left_proj, out, sems.at[0]).wait()


def head_kernel(sectors, band, kept, boundary, right, row_tensor, left_proj, first, wide, r, *refs):
    lefts, (x, rp, raw, r32, rp32, h, sems) = refs[: sectors - 1], refs[sectors - 1 :]
    layer = load(row_tensor.at[0, 0], raw, sems.at[0])
    copies = [send_block(kept, s, left_proj, lefts[s - 1], sems.at[s]) for s in range(1, sectors)]

    @pl.when(band[0] == 0)
    def _():
        a = load(right.at[0, 0, 0], rp, sems.at[sectors])
        b = load(boundary.at[0, 0], x, sems.at[sectors + 1])
        a.wait()
        b.wait()
        contract_right(x, rp, rp32, h)

    layer.wait()
    spread_layer(raw, r32, r)

    @pl.when(band[0] == 0)
    def _():
        contract_layer(r, h, wide)

    for copy in copies:
        copy.wait()


def tail_kernel(s, band, kept, left, wide, state, lpt, acc):
    @pl.when(band[0] == 0)
    def _():
        flip_left(left, lpt)
        contract_left(lpt, wide, acc, live=live_mask(left, kept[0, 0, s]))
        store(acc, [state])


def upper_kernel(s, n_out, band, kept, before, boundary, right, r, left, *refs):
    outs, (rp32, h, w, lpt, acc) = refs[:n_out], refs[n_out:]

    @pl.when(band[0] == 0)
    def _():
        contract_right(boundary.at[0, s], right.at[0, 0, s], rp32, h)
        contract_layer(r, h, w)
        flip_left(left, lpt)
        contract_left(lpt, w, acc, live=live_mask(left, kept[0, 0, s]))
        store(acc, outs)


def lower_kernel(s, part, parts, carried, band, kept, *refs):
    refs = list(refs)
    refs.pop(0)
    before = refs.pop(0) if carried else None
    own = [refs.pop(0) for _ in range(parts if part == parts - 1 else 0)]
    arrived, right, r, left, out = (refs.pop(0) for _ in range(5))
    rp32, h, w, lpt, acc, block, sem = refs
    n = arrived.shape[0]
    last = part == parts - 1

    if last:
        target = out.at[0, 0, s]

        @pl.when(band[0] == 0)
        def _():
            copies, at = [], 0
            for i, piece in enumerate(own):
                copies.append(load(piece, target.at[pl.ds(at, piece.shape[0])], sem.at[i]))
                at += piece.shape[0]
            for copy in copies:
                copy.wait()

    @pl.when(band[0] == 1)
    def _():
        contract_right(arrived, right.at[0, 0, s], rp32, h)
        contract_layer(r, h, w)
        flip_left(left, lpt)
        half = lpt.at[:, pl.ds(part * n * h.shape[0], n * h.shape[0])]
        live = live_mask(left, kept[0, 0, s]) if last else None
        contract_left(half, w, acc if last else out, carried=before, live=live)
        if last:
            store(acc, [block])
            pltpu.sync_copy(block, target)


def body(boundary, row_tensor, right_proj, left_proj, kept):
    _, sectors, W, D, _ = boundary.shape
    band = lax.axis_index("band").astype(jnp.int32)[None]
    cols = shift_pairs(lax.axis_size("col"))
    down = [(0, 1), (1, 0)]
    splits = [1] * (sectors - 1) + [2]

    block = pltpu.VMEM((W, D, W), BF16)
    ext = pltpu.VMEM((W + 1, D, W), BF16)
    layer = pltpu.VMEM((D * D, D * D), BF16)
    wide_shape = pltpu.VMEM((D, W, D, W), BF16)
    rp32, lpt, acc = pltpu.VMEM((W * D, W), F32), pltpu.VMEM((W, W * D), BF16), pltpu.VMEM((W * D, W), F32)

    def wide_part(n):
        return pltpu.VMEM((D, n, D, W), BF16)

    def cost(part):
        return pl.CostEstimate(
            flops=int(8 * part * W * D * W * W * D), bytes_accessed=8 * W * D * W, transcendentals=0
        )

    def call(kernel, name, part, in_specs, outs, scratch, **kw):
        single = len(outs) == 1
        specs = [ANY if isinstance(o, jax.ShapeDtypeStruct) else VMEM for o in outs]
        return pl.pallas_call(
            kernel, out_shape=outs[0] if single else outs, in_specs=in_specs,
            out_specs=specs[0] if single else specs, scratch_shapes=scratch,
            compiler_params=PARAMS, cost_estimate=cost(part), name=name, **kw,
        )

    dma = pltpu.SemaphoreType.DMA((sectors + 2,))
    first = call(first_kernel, "first", 0.1, [SMEM, HBM], [ext], [dma])(kept, in_hbm(left_proj))
    left = [lax.ppermute(first, "col", cols)]
    wide, r, *sends = call(
        functools.partial(head_kernel, sectors), "head", 0.75,
        [SMEM, SMEM] + [HBM] * 4 + [ANY], [wide_shape, layer] + [ext] * (sectors - 1),
        [block, block, pltpu.VMEM((D, D, D, D), BF16), pltpu.VMEM((D * D * D * D // W, W), F32), rp32, wide_shape, dma],
    )(band, kept, in_hbm(boundary), in_hbm(right_proj), in_hbm(row_tensor), in_hbm(left_proj), first)
    left += [lax.ppermute(send, "col", cols) for send in sends]
    left = [in_vmem(x) for x in left]
    states = [[
        call(functools.partial(tail_kernel, 0), "tail", 0.25, [SMEM, SMEM, VMEM, VMEM], [block], [lpt, acc])(
            band, kept, left[0], in_vmem(wide)
        )
    ]]
    arrived = [[lax.ppermute(states[0][0], "band", down)]]
    r = in_vmem(r)
    near, right = in_vmem(boundary), in_vmem(right_proj)
    for s in range(1, sectors):
        k = splits[s]
        outs = call(
            functools.partial(upper_kernel, s, k), "upper", 1, [SMEM, SMEM, ANY] + [VMEM] * 4,
            [pltpu.VMEM((W // k, D, W), BF16)] * k, [rp32, wide_part(W), wide_part(W), lpt, acc],
        )(band, kept, states[s - 1][0], near, right, r, left[s])
        states.append(list(outs) if k > 1 else [outs])
        arrived.append([lax.ppermute(x, "band", down) for x in states[s]])
    result = None
    for s in range(sectors):
        k = splits[s]
        total = None
        for part in range(k):
            last = part == k - 1
            aliased = last and result is not None
            operands, specs = [states[-1][-1] if result is None else result], [ANY]
            if result is not None and not last:
                operands, specs = [in_hbm(result)], [HBM]
            if total is not None:
                operands.append(in_vmem(total))
                specs.append(VMEM)
            if last:
                operands += [in_vmem(x) for x in states[s]]
                specs += [VMEM] * k
            operands += [in_vmem(arrived[s][part]), right, r, left[s]]
            specs += [VMEM] * 4
            out = jax.ShapeDtypeStruct((1, 1, sectors, W, D, W), BF16) if last else acc
            done = call(
                functools.partial(lower_kernel, s, part, k, total is not None), "lower", 1 / k,
                [SMEM, SMEM] + specs, [out],
                [rp32, wide_part(W // k), wide_part(W // k), lpt, acc, block, dma],
                input_output_aliases={2: 0} if aliased else {},
            )(band, kept, *operands)
            if last:
                result = done
            else:
                total = done
    return result


def solution(mesh):
    in_specs = (
        P("col", None, None, None, None),
        P("band", "col", None, None, None, None),
        P("band", "col", None, None, None, None),
        P("band", "col", None, None, None, None),
        P("band", "col", None),
    )
    out_specs = P("band", "col", None, None, None, None)
    return jax.shard_map(body, mesh=mesh, in_specs=in_specs, out_specs=out_specs, check_vma=False)
```

```python
import functools

import jax
import jax.numpy as jnp
from jax import lax
from jax.experimental import pallas as pl
from jax.experimental.pallas import tpu as pltpu
from jax.sharding import PartitionSpec as P

F32, BF16 = jnp.float32, jnp.bfloat16
ANY = pl.BlockSpec(memory_space=pl.ANY)
HBM = pl.BlockSpec(memory_space=pltpu.HBM)
SMEM = pl.BlockSpec(memory_space=pltpu.SMEM)
VMEM = pl.BlockSpec(memory_space=pltpu.VMEM)
PARAMS = pltpu.CompilerParams(vmem_limit_bytes=28 << 20)


X, Y_HI, Z, CORES, BANDS = 4, 2, 8, 2, 2
COLS = X * Y_HI * Z * CORES


def place(column, band):
    return column * BANDS + band


def straight():
    return [(place((c - 1) % COLS, b), place(c, b)) for c in range(COLS) for b in range(BANDS)]


def around():
    first, second = [], []
    for c in range(COLS):
        for b in range(BANDS):
            here, there = place(c, b), place((c + 1) % COLS, b)
            if (c + 1) % (Z * CORES):
                first.append((here, there))
                second.append((there, there))
            else:
                x, y_hi = divmod(c // (Z * CORES), Y_HI)
                y = (y_hi * BANDS + b - 1) % (Y_HI * BANDS)
                via = place((x * Y_HI + y // BANDS) * Z * CORES, y % BANDS)
                first.append((here, via))
                second.append((via, there))
    return first, second


def in_vmem(array):
    return pltpu.with_memory_space_constraint(array, pltpu.VMEM)


def in_hbm(array):
    return pltpu.with_memory_space_constraint(array, pltpu.HBM)


def contract_right(x, rp, rp32, h, at=0):
    n, D, W = x.shape
    rp32[...] = rp[...].reshape(W * D, W).astype(F32)
    rows = x[...].reshape(n * D, W)
    for t in range(0, D, 2):
        pair = [rp32[pl.ds(t + i, W, stride=D), :].astype(BF16) for i in range(2)]
        y = jnp.dot(rows, jnp.concatenate(pair, axis=1), preferred_element_type=F32).astype(BF16)
        h[t, at : at + n] = y[:, :W].reshape(n, D, W)
        h[t + 1, at : at + n] = y[:, W:].reshape(n, D, W)


def contract_layer(r, h, w, at=0, n=None):
    D, W = h.shape[0], h.shape[-1]
    n = h.shape[1] if n is None else n
    layer = r[...]

    def step(i, _):
        a = at + 2 * i
        pair = [h[:, a + k].reshape(D * D, W) for k in range(2)]
        y = jnp.dot(layer, jnp.concatenate(pair, axis=1), preferred_element_type=F32).astype(BF16)
        for k in range(2):
            w[:, a + k] = y[:, k * W : (k + 1) * W].reshape(D, D, W)
        return 0

    lax.fori_loop(0, n // 2, step, 0, unroll=32)


def flip_left(lp, lpt):
    D, W = lp.shape[1:]
    lpt[...] = lp[:W].reshape(W * D, W).T


def live_mask(lp, keep_right):
    W = lp.shape[-1]
    keep_left = lp[W, 0:1, :].astype(F32)
    rows = lax.broadcasted_iota(jnp.int32, (W, W), 0).astype(F32)
    lanes = lax.broadcasted_iota(jnp.int32, (W, W), 1)
    return (rows < keep_left) & (lanes < keep_right)


def contract_left(lpt, w, acc, at=0, n=None, carried=None, live=None):
    D, W = w.shape[0], w.shape[-1]
    n = w.shape[1] if n is None else n
    left = lpt[:, at * D : (at + n) * D]
    for q in range(0, D, 2):
        pair = [w[q + k, at : at + n].reshape(n * D, W) for k in range(2)]
        y = jnp.dot(left, jnp.concatenate(pair, axis=1), preferred_element_type=F32)
        for k in range(2):
            rows = pl.ds(q + k, W, stride=D)
            z = y[:, k * W : (k + 1) * W]
            if carried is not None:
                z = z + carried[rows, :]
            if live is not None:
                z = jnp.where(live, z, 0.0)
            acc[rows, :] = z


def store(acc, outs):
    at = 0
    for out in outs:
        n, D, W = out.shape
        out[...] = acc[at * D : (at + n) * D, :].astype(BF16).reshape(out.shape)
        at += n


def spread_layer(raw, r32, r):
    D = raw.shape[0]
    rows = lax.broadcasted_iota(jnp.int32, (D, D * D), 0)
    lanes = lax.broadcasted_iota(jnp.int32, (D, D * D), 1)
    total = jnp.zeros((D * D, D * D), F32)
    for p in range(D):
        place = (lanes == rows * D + p).astype(BF16)
        total += jnp.dot(raw[:, p].reshape(D * D, D), place, preferred_element_type=F32)
    n, W = D * D, r32.shape[1]
    for i in range(n // W):
        r32[i * n : (i + 1) * n, :] = total[:, i * W : (i + 1) * W]
        for q in range(D):
            r[q * D : (q + 1) * D, i * W : (i + 1) * W] = r32[pl.ds(i * n + q, D, stride=D), :].astype(BF16)


def load(src, dst, sem):
    copy = pltpu.make_async_copy(src, dst, sem)
    copy.start()
    return copy


def send_block(s, left_proj, out, sem):
    return load(left_proj.at[0, 0, s], out.at[pl.ds(0, left_proj.shape[3])], sem)


def add_kept(kept, s, out):
    out[out.shape[0] - 1] = jnp.full(out.shape[1:], kept[0, 0, s].astype(F32), F32).astype(BF16)


def first_kernel(kept_in, left_proj, out, kept, sems):
    counts = load(kept_in, kept, sems.at[1])
    copy = send_block(0, left_proj, out, sems.at[0])
    counts.wait()
    add_kept(kept, 0, out)
    copy.wait()


def head_kernel(band, kept, boundary, right, row_tensor, left_proj, first, wide, r, left, x, rp, raw, r32, rp32, h, sems):
    layer = load(row_tensor.at[0, 0], raw, sems.at[0])
    copy = send_block(1, left_proj, left, sems.at[1])
    add_kept(kept, 1, left)

    @pl.when(band[0] == 0)
    def _():
        a = load(right.at[0, 0, 0], rp, sems.at[2])
        b = load(boundary.at[0, 0], x, sems.at[3])
        a.wait()
        b.wait()
        contract_right(x, rp, rp32, h)

    layer.wait()
    spread_layer(raw, r32, r)

    @pl.when(band[0] == 0)
    def _():
        contract_layer(r, h, wide)

    copy.wait()


def wide_kernel(s, n_before, band, *refs):
    boundary, right, r, wide, rp32, h = refs[n_before:]

    @pl.when(band[0] == 0)
    def _():
        contract_right(boundary.at[0, s], right.at[0, 0, s], rp32, h)
        contract_layer(r, h, wide)


def tail_kernel(s, n_out, sends, band, kept, left, wide, *refs):
    refs = list(refs)
    left_proj = refs.pop(0) if sends else None
    outs = [refs.pop(0) for _ in range(n_out)]
    send = refs.pop(0) if sends else None
    lpt, acc, sems = refs
    if sends:
        copy = send_block(s + 2, left_proj, send, sems.at[0])
        add_kept(kept, s + 2, send)

    @pl.when(band[0] == 0)
    def _():
        flip_left(left, lpt)
        contract_left(lpt, wide, acc, live=live_mask(left, kept[0, 0, s]))
        store(acc, outs)

    if sends:
        copy.wait()


def lower_kernel(s, part, parts, carried, n_before, band, kept, *refs):
    refs = list(refs[n_before:])
    before = refs.pop(0) if carried else None
    own = [refs.pop(0) for _ in range(parts if part == parts - 1 else 0)]
    arrived, right, r, left, out = (refs.pop(0) for _ in range(5))
    rp32, h, w, lpt, acc, block, sem = refs
    n = arrived.shape[0]
    last = part == parts - 1

    if last:
        target = out.at[0, 0, s]

        @pl.when(band[0] == 0)
        def _():
            copies, at = [], 0
            for i, piece in enumerate(own):
                copies.append(load(piece, target.at[pl.ds(at, piece.shape[0])], sem.at[i]))
                at += piece.shape[0]
            for copy in copies:
                copy.wait()

    @pl.when(band[0] == 1)
    def _():
        contract_right(arrived, right.at[0, 0, s], rp32, h)
        contract_layer(r, h, w)
        flip_left(left, lpt)
        half = lpt.at[:, pl.ds(part * n * h.shape[0], n * h.shape[0])]
        live = live_mask(left, kept[0, 0, s]) if last else None
        contract_left(half, w, acc if last else out, carried=before, live=live)
        if last:
            store(acc, [block])
            pltpu.sync_copy(block, target)


def body(boundary, row_tensor, right_proj, left_proj, kept):
    _, sectors, W, D, _ = boundary.shape
    band = lax.axis_index("band").astype(jnp.int32)[None]
    down = [(0, 1)]
    splits = [1] * (sectors - 1) + [2]

    block = pltpu.VMEM((W, D, W), BF16)
    ext = pltpu.VMEM((W + 1, D, W), BF16)
    layer = pltpu.VMEM((D * D, D * D), BF16)
    wide_shape = pltpu.VMEM((D, W, D, W), BF16)
    rp32, lpt, acc = pltpu.VMEM((W * D, W), F32), pltpu.VMEM((W, W * D), BF16), pltpu.VMEM((W * D, W), F32)

    def wide_part(n):
        return pltpu.VMEM((D, n, D, W), BF16)

    def cost(part):
        return pl.CostEstimate(
            flops=int(8 * part * W * D * W * W * D), bytes_accessed=8 * W * D * W, transcendentals=0
        )

    def call(kernel, name, part, in_specs, outs, scratch, **kw):
        single = len(outs) == 1
        specs = [ANY if isinstance(o, jax.ShapeDtypeStruct) else VMEM for o in outs]
        return pl.pallas_call(
            kernel, out_shape=outs[0] if single else outs, in_specs=in_specs,
            out_specs=specs[0] if single else specs, scratch_shapes=scratch,
            compiler_params=PARAMS, cost_estimate=cost(part), name=name, **kw,
        )

    dma = pltpu.SemaphoreType.DMA((4,))
    direct, (hop, rest) = straight(), around()
    axes = ("col", "band")
    first = call(first_kernel, "first", 0.1, [HBM, HBM], [ext], [pltpu.SMEM(kept.shape, jnp.int32), dma])(
        in_hbm(kept), in_hbm(left_proj)
    )
    left = [in_vmem(lax.ppermute(first, axes, direct))]
    wide, r, send = call(
        head_kernel, "head", 0.75, [SMEM, SMEM] + [HBM] * 4 + [ANY], [wide_shape, layer, ext],
        [block, block, pltpu.VMEM((D, D, D, D), BF16), pltpu.VMEM((D * D * D * D // W, W), F32), rp32, wide_shape, dma],
    )(band, kept, in_hbm(boundary), in_hbm(right_proj), in_hbm(row_tensor), in_hbm(left_proj), first)
    r, near, right = in_vmem(r), in_vmem(boundary), in_vmem(right_proj)
    states, arrived, result = [], [], None

    def tail(s, wide, sends=False):
        k, extra = splits[s], [in_hbm(left_proj)] if sends else []
        outs = call(
            functools.partial(tail_kernel, s, k, sends), "tail", 0.25, [SMEM, SMEM, VMEM, VMEM] + [HBM] * len(extra),
            [pltpu.VMEM((W // k, D, W), BF16)] * k + [ext] * len(extra), [lpt, acc, dma],
        )(band, kept, left[s], in_vmem(wide), *extra)
        outs = list(outs) if isinstance(outs, (list, tuple)) else [outs]
        states.append(outs[:k])
        arrived.append([lax.ppermute(x, "band", down) for x in outs[:k]])
        return outs[k:]

    def widen(s, before, result=None):
        return call(
            functools.partial(wide_kernel, s, len(before)), "wide", 0.75,
            [SMEM] + [HBM if x is result else ANY for x in before] + [VMEM] * 3, [wide_shape], [rp32, wide_shape],
        )(band, *[in_hbm(x) if x is result else x for x in before], near, right, r)

    def lower(s, result, after):
        k = splits[s]
        total = None
        for part in range(k):
            last = part == k - 1
            operands, specs = list(after), [ANY] * len(after)
            aliases = {}
            if result is not None and last:
                operands, specs, aliases = [result] + operands, [ANY] + specs, {2: 0}
            elif result is not None:
                operands, specs = [in_hbm(result)] + operands, [HBM] + specs
            n_before = len(operands)
            if total is not None:
                operands.append(in_vmem(total))
                specs.append(VMEM)
            if last:
                operands += [in_vmem(x) for x in states[s]]
                specs += [VMEM] * k
            operands += [in_vmem(arrived[s][part]), right, r, left[s]]
            specs += [VMEM] * 4
            out = jax.ShapeDtypeStruct((1, 1, sectors, W, D, W), BF16) if last else acc
            total = call(
                functools.partial(lower_kernel, s, part, k, total is not None, n_before), "lower", 1 / k,
                [SMEM, SMEM] + specs, [out],
                [rp32, wide_part(W // k), wide_part(W // k), lpt, acc, block, dma], input_output_aliases=aliases,
            )(band, kept, *operands)
        return total

    left.append(in_vmem(lax.ppermute(send, axes, direct)))
    (send,) = tail(0, wide, True)
    part_way = lax.ppermute(send, axes, hop)
    wide = widen(1, [states[0][0]])
    tail(1, wide)
    part_way, states[1][0] = lax.optimization_barrier((part_way, states[1][0]))
    result = lower(0, None, [states[1][0]])
    left.append(in_vmem(lax.ppermute(part_way, axes, rest)))
    wide = widen(2, [part_way, result], result)
    tail(2, wide)
    result = lower(1, result, [states[2][0]])
    return lower(2, result, [])


def solution(mesh):
    in_specs = (
        P("col", None, None, None, None),
        P("band", "col", None, None, None, None),
        P("band", "col", None, None, None, None),
        P("band", "col", None, None, None, None),
        P("band", "col", None),
    )
    out_specs = P("band", "col", None, None, None, None)
    return jax.shard_map(body, mesh=mesh, in_specs=in_specs, out_specs=out_specs, check_vma=False)
```

```python
import functools

import jax
import jax.numpy as jnp
from jax import lax
from jax.experimental import pallas as pl
from jax.experimental.pallas import tpu as pltpu
from jax.sharding import PartitionSpec as P

F32, BF16 = jnp.float32, jnp.bfloat16
ANY = pl.BlockSpec(memory_space=pl.ANY)
HBM = pl.BlockSpec(memory_space=pltpu.HBM)
SMEM = pl.BlockSpec(memory_space=pltpu.SMEM)
VMEM = pl.BlockSpec(memory_space=pltpu.VMEM)
PARAMS = pltpu.CompilerParams(vmem_limit_bytes=28 << 20)


X, Y_HI, Z, CORES, BANDS = 4, 2, 8, 2, 2
COLS = X * Y_HI * Z * CORES


def place(column, band):
    return column * BANDS + band


def straight():
    return [(place((c - 1) % COLS, b), place(c, b)) for c in range(COLS) for b in range(BANDS)]


def around():
    first, second = [], []
    for c in range(COLS):
        for b in range(BANDS):
            here, there = place(c, b), place((c + 1) % COLS, b)
            if (c + 1) % (Z * CORES):
                first.append((here, there))
                second.append((there, there))
            else:
                x, y_hi = divmod(c // (Z * CORES), Y_HI)
                y = (y_hi * BANDS + b - 1) % (Y_HI * BANDS)
                via = place((x * Y_HI + y // BANDS) * Z * CORES, y % BANDS)
                first.append((here, via))
                second.append((via, there))
    return first, second


def in_vmem(array):
    return pltpu.with_memory_space_constraint(array, pltpu.VMEM)


def in_hbm(array):
    return pltpu.with_memory_space_constraint(array, pltpu.HBM)


def flip_right(rp, rp32, rpt):
    W, D, _ = rp.shape
    rp32[...] = rp[...].reshape(W * D, W).astype(F32)
    for t in range(D):
        rpt[t // 2, :, (t % 2) * W : (t % 2 + 1) * W] = rp32[pl.ds(t, W, stride=D), :].astype(BF16)


def contract_right(x, rpt, h):
    n, D, W = x.shape
    rows = x[...].reshape(n * D, W)
    for t in range(0, D, 2):
        y = jnp.dot(rows, rpt[t // 2], preferred_element_type=F32).astype(BF16)
        h[t] = y[:, :W].reshape(n, D, W)
        h[t + 1] = y[:, W:].reshape(n, D, W)


def contract_layer(r, h, w, at=0, n=None):
    D, W = h.shape[0], h.shape[-1]
    n = h.shape[1] if n is None else n
    layer = r[...]

    def step(i, _):
        a = at + 2 * i
        pair = [h[:, a + k].reshape(D * D, W) for k in range(2)]
        y = jnp.dot(layer, jnp.concatenate(pair, axis=1), preferred_element_type=F32).astype(BF16)
        for k in range(2):
            w[:, a + k] = y[:, k * W : (k + 1) * W].reshape(D, D, W)
        return 0

    lax.fori_loop(0, n // 2, step, 0, unroll=32)


def flip_left(lp, lpt):
    D, W = lp.shape[1:]
    lpt[...] = lp[:W].reshape(W * D, W).T


def live_mask(lp, keep_right):
    W = lp.shape[-1]
    keep_left = lp[W, 0:1, :].astype(F32)
    rows = lax.broadcasted_iota(jnp.int32, (W, W), 0).astype(F32)
    lanes = lax.broadcasted_iota(jnp.int32, (W, W), 1)
    return (rows < keep_left) & (lanes < keep_right)


def contract_left(lpt, w, acc, at=0, n=None, carried=None, live=None):
    D, W = w.shape[0], w.shape[-1]
    n = w.shape[1] if n is None else n
    left = lpt[:, at * D : (at + n) * D]
    for q in range(0, D, 2):
        pair = [w[q + k, at : at + n].reshape(n * D, W) for k in range(2)]
        y = jnp.dot(left, jnp.concatenate(pair, axis=1), preferred_element_type=F32)
        for k in range(2):
            rows = pl.ds(q + k, W, stride=D)
            z = y[:, k * W : (k + 1) * W]
            if carried is not None:
                z = z + carried[rows, :]
            if live is not None:
                z = jnp.where(live, z, 0.0)
            acc[rows, :] = z


def store(acc, outs):
    at = 0
    for out in outs:
        n, D, W = out.shape
        out[...] = acc[at * D : (at + n) * D, :].astype(BF16).reshape(out.shape)
        at += n


def spread_layer(raw, r32, r):
    D = raw.shape[0]
    rows = lax.broadcasted_iota(jnp.int32, (D, D * D), 0)
    lanes = lax.broadcasted_iota(jnp.int32, (D, D * D), 1)
    total = jnp.zeros((D * D, D * D), F32)
    for p in range(D):
        place = (lanes == rows * D + p).astype(BF16)
        total += jnp.dot(raw[:, p].reshape(D * D, D), place, preferred_element_type=F32)
    n, W = D * D, r32.shape[1]
    for i in range(n // W):
        r32[i * n : (i + 1) * n, :] = total[:, i * W : (i + 1) * W]
        for q in range(D):
            r[q * D : (q + 1) * D, i * W : (i + 1) * W] = r32[pl.ds(i * n + q, D, stride=D), :].astype(BF16)


def load(src, dst, sem):
    copy = pltpu.make_async_copy(src, dst, sem)
    copy.start()
    return copy


def send_block(s, left_proj, out, sem):
    return load(left_proj.at[0, 0, s], out.at[pl.ds(0, left_proj.shape[3])], sem)


def add_kept(kept, s, out):
    out[out.shape[0] - 1] = jnp.full(out.shape[1:], kept[0, 0, s].astype(F32), F32).astype(BF16)


def first_kernel(kept_in, left_proj, out, kept, sems):
    counts = load(kept_in, kept, sems.at[1])
    copy = send_block(0, left_proj, out, sems.at[0])
    counts.wait()
    add_kept(kept, 0, out)
    copy.wait()


def head_kernel(band, kept, boundary, right, row_tensor, left_proj, first, wide, r, left, x, rp, raw, r32, rp32, rpt, h, sems):
    layer = load(row_tensor.at[0, 0], raw, sems.at[0])
    copy = send_block(1, left_proj, left, sems.at[1])
    add_kept(kept, 1, left)

    @pl.when(band[0] == 0)
    def _():
        a = load(right.at[0, 0, 0], rp, sems.at[2])
        b = load(boundary.at[0, 0], x, sems.at[3])
        a.wait()
        flip_right(rp, rp32, rpt)
        b.wait()
        contract_right(x, rpt, h)

    layer.wait()
    spread_layer(raw, r32, r)

    @pl.when(band[0] == 0)
    def _():
        contract_layer(r, h, wide)

    copy.wait()


def wide_kernel(s, n_before, prepares, band, *refs):
    refs = list(refs[n_before:])
    boundary, right, r, wide = (refs.pop(0) for _ in range(4))
    ahead = refs.pop(0) if prepares else None
    rp32, rpt, h = refs

    @pl.when(band[0] == 0)
    def _():
        flip_right(right.at[0, 0, s], rp32, rpt)
        contract_right(boundary.at[0, s], rpt, h)
        contract_layer(r, h, wide)

    if prepares:

        @pl.when(band[0] == 1)
        def _():
            for k in range(right.shape[2]):
                flip_right(right.at[0, 0, k], rp32, ahead.at[k])


def tail_kernel(s, n_out, sends, band, kept, left, wide, *refs):
    refs = list(refs)
    left_proj = refs.pop(0) if sends else None
    outs = [refs.pop(0) for _ in range(n_out)]
    lpt = refs.pop(0)
    send = refs.pop(0) if sends else None
    acc, sems = refs
    if sends:
        copy = send_block(s + 2, left_proj, send, sems.at[0])
        add_kept(kept, s + 2, send)
    flip_left(left, lpt)

    @pl.when(band[0] == 0)
    def _():
        contract_left(lpt, wide, acc, live=live_mask(left, kept[0, 0, s]))
        store(acc, outs)

    if sends:
        copy.wait()


def lower_kernel(s, part, parts, carried, n_before, band, kept, *refs):
    refs = list(refs[n_before:])
    before = refs.pop(0) if carried else None
    arrived, rpt, r, left, lpt, out, h, w, acc = refs
    n = arrived.shape[0]
    last = part == parts - 1

    @pl.when(band[0] == 1)
    def _():
        contract_right(arrived, rpt.at[s], h)
        contract_layer(r, h, w)
        half = lpt.at[:, pl.ds(part * n * h.shape[0], n * h.shape[0])]
        live = live_mask(left, kept[0, 0, s]) if last else None
        contract_left(half, w, acc if last else out, carried=before, live=live)
        if last:
            store(acc, [out])


def end_kernel(s, part, own_places, band, kept, *refs):
    refs = list(refs)
    own = [refs.pop(0) for _ in own_places]
    done = [refs.pop(0) for _ in range(s)]
    before, arrived, rpt, r, left, lpt, out, h, w, acc, block, sems = refs
    n, D, W = arrived.shape

    @pl.when(band[0] == 0)
    def _():
        copies = [
            load(piece, out.at[0, 0, k, pl.ds(at, piece.shape[0])], sems.at[i])
            for i, (piece, (k, at)) in enumerate(zip(own, own_places))
        ]
        for copy in copies:
            copy.wait()

    @pl.when(band[0] == 1)
    def _():
        copies = [load(piece, out.at[0, 0, k], sems.at[k]) for k, piece in enumerate(done)]
        contract_right(arrived, rpt.at[s], h)
        contract_layer(r, h, w)
        half = lpt.at[:, pl.ds(part * n * D, n * D)]
        contract_left(half, w, acc, carried=before, live=live_mask(left, kept[0, 0, s]))
        step = block.shape[0] // 4
        for i in range(4):
            rows = pl.ds(i * step, step)
            block[rows] = acc[i * step * D : (i + 1) * step * D, :].astype(BF16).reshape(step, D, W)
            copies.append(load(block.at[rows], out.at[0, 0, s, rows], sems.at[s + i]))
        for copy in copies:
            copy.wait()


def body(boundary, row_tensor, right_proj, left_proj, kept):
    _, sectors, W, D, _ = boundary.shape
    band = lax.axis_index("band").astype(jnp.int32)[None]
    down = [(0, 1)]
    splits = [2] + [1] * (sectors - 2) + [2]

    block = pltpu.VMEM((W, D, W), BF16)
    ext = pltpu.VMEM((W + 1, D, W), BF16)
    layer = pltpu.VMEM((D * D, D * D), BF16)
    wide_shape = pltpu.VMEM((D, W, D, W), BF16)
    rp32, lpt, acc = pltpu.VMEM((W * D, W), F32), pltpu.VMEM((W, W * D), BF16), pltpu.VMEM((W * D, W), F32)

    def wide_part(n):
        return pltpu.VMEM((D, n, D, W), BF16)

    def cost(part):
        return pl.CostEstimate(
            flops=int(8 * part * W * D * W * W * D), bytes_accessed=8 * W * D * W, transcendentals=0
        )

    def call(kernel, name, part, in_specs, outs, scratch, **kw):
        single = len(outs) == 1
        specs = [ANY if isinstance(o, jax.ShapeDtypeStruct) else VMEM for o in outs]
        return pl.pallas_call(
            kernel, out_shape=outs[0] if single else outs, in_specs=in_specs,
            out_specs=specs[0] if single else specs, scratch_shapes=scratch,
            compiler_params=PARAMS, cost_estimate=cost(part), name=name, **kw,
        )

    rpt = pltpu.VMEM((D // 2, W, 2 * W), BF16)
    dma = pltpu.SemaphoreType.DMA((sectors + 4,))
    direct, (hop, rest) = straight(), around()
    axes = ("col", "band")
    first = call(first_kernel, "first", 0.1, [HBM, HBM], [ext], [pltpu.SMEM(kept.shape, jnp.int32), dma])(
        in_hbm(kept), in_hbm(left_proj)
    )
    left = [in_vmem(lax.ppermute(first, axes, direct))]
    wide, r, send = call(
        head_kernel, "head", 0.75, [SMEM, SMEM] + [HBM] * 4 + [ANY], [wide_shape, layer, ext],
        [block, block, pltpu.VMEM((D, D, D, D), BF16), pltpu.VMEM((D * D * D * D // W, W), F32), rp32, rpt, wide_shape, dma],
    )(band, kept, in_hbm(boundary), in_hbm(right_proj), in_hbm(row_tensor), in_hbm(left_proj), first)
    r, near, right = in_vmem(r), in_vmem(boundary), in_vmem(right_proj)
    states, arrived, flipped = [], [], []

    def tail(s, wide, sends=False):
        k, extra = splits[s], [in_hbm(left_proj)] if sends else []
        outs = call(
            functools.partial(tail_kernel, s, k, sends), "tail", 0.25, [SMEM, SMEM, VMEM, VMEM] + [HBM] * len(extra),
            [pltpu.VMEM((W // k, D, W), BF16)] * k + [lpt] + [ext] * len(extra), [acc, dma],
        )(band, kept, left[s], in_vmem(wide), *extra)
        states.append(list(outs[:k]))
        flipped.append(in_vmem(outs[k]))
        arrived.append([])
        return outs[k + 1 :]

    def give(s, part=0):
        arrived[s].append(lax.ppermute(states[s][part], "band", down))

    def widen(s, before, prepares=False):
        return call(
            functools.partial(wide_kernel, s, len(before), prepares), "wide", 0.75,
            [SMEM] + [ANY] * len(before) + [VMEM] * 3,
            [wide_shape] + ([pltpu.VMEM((sectors, *rpt.shape), BF16)] if prepares else []), [rp32, rpt, wide_shape],
        )(band, *before, near, right, r)

    def lower(s, part, before, total=None):
        k = splits[s]
        carried = [] if total is None else [in_vmem(total)]
        operands = carried + [in_vmem(arrived[s][part]), ahead, r, left[s], flipped[s]]
        return call(
            functools.partial(lower_kernel, s, part, k, bool(carried), len(before)), "lower", 1 / k,
            [SMEM, SMEM] + [ANY] * len(before) + [VMEM] * len(operands), [block if part == k - 1 else acc],
            [wide_part(W // k), wide_part(W // k), acc],
        )(band, kept, *before, *operands)

    left.append(in_vmem(lax.ppermute(send, axes, direct)))
    (send,) = tail(0, wide, True)
    give(0)
    part_way = lax.ppermute(send, axes, hop)
    wide, ahead = widen(1, [states[0][0]], True)
    states[0][1], wide = lax.optimization_barrier((states[0][1], wide))
    give(0, 1)
    ahead = in_vmem(ahead)
    tail(1, wide)
    give(1)
    part_way, states[1][0] = lax.optimization_barrier((part_way, states[1][0]))
    left.append(in_vmem(lax.ppermute(part_way, axes, rest)))
    wide = widen(2, [part_way])
    done = [lower(0, 1, [], lower(0, 0, [wide]))]
    tail(2, wide)
    give(2)
    give(2, 1)
    done.append(lower(1, 0, [states[2][0], done[0]]))
    s, k = sectors - 1, splits[-1]
    total = lower(s, 0, [done[1]])
    own = [x for state in states for x in state]
    places = [(i, W // splits[i] * j) for i in range(sectors) for j in range(splits[i])]
    operands = own + done + [total, arrived[s][k - 1]]
    return call(
        functools.partial(end_kernel, s, k - 1, places), "end", 1 / k, [SMEM, SMEM] + [VMEM] * (len(operands) + 4),
        [jax.ShapeDtypeStruct((1, 1, sectors, W, D, W), BF16)],
        [wide_part(W // k), wide_part(W // k), acc, block, dma],
    )(band, kept, *[in_vmem(x) for x in operands], ahead, r, left[s], flipped[s])


def solution(mesh):
    in_specs = (
        P("col", None, None, None, None),
        P("band", "col", None, None, None, None),
        P("band", "col", None, None, None, None),
        P("band", "col", None, None, None, None),
        P("band", "col", None),
    )
    out_specs = P("band", "col", None, None, None, None)
    return jax.shard_map(body, mesh=mesh, in_specs=in_specs, out_specs=out_specs, check_vma=False)
```

```python
import functools

import jax
import jax.numpy as jnp
from jax import lax
from jax.experimental import pallas as pl
from jax.experimental.pallas import tpu as pltpu
from jax.sharding import PartitionSpec as P

F32, BF16 = jnp.float32, jnp.bfloat16
ANY = pl.BlockSpec(memory_space=pl.ANY)
HBM = pl.BlockSpec(memory_space=pltpu.HBM)
SMEM = pl.BlockSpec(memory_space=pltpu.SMEM)
VMEM = pl.BlockSpec(memory_space=pltpu.VMEM)
PARAMS = pltpu.CompilerParams(vmem_limit_bytes=28 << 20)


X, Y_HI, Z, CORES, BANDS = 4, 2, 8, 2, 2
COLS = X * Y_HI * Z * CORES


def place(column, band):
    return column * BANDS + band


def straight():
    return [(place((c - 1) % COLS, b), place(c, b)) for c in range(COLS) for b in range(BANDS)]


def around():
    first, second = [], []
    for c in range(COLS):
        for b in range(BANDS):
            here, there = place(c, b), place((c + 1) % COLS, b)
            if (c + 1) % (Z * CORES):
                first.append((here, there))
                second.append((there, there))
            else:
                x, y_hi = divmod(c // (Z * CORES), Y_HI)
                y = (y_hi * BANDS + b - 1) % (Y_HI * BANDS)
                via = place((x * Y_HI + y // BANDS) * Z * CORES, y % BANDS)
                first.append((here, via))
                second.append((via, there))
    return first, second


def in_vmem(array):
    return pltpu.with_memory_space_constraint(array, pltpu.VMEM)


def in_hbm(array):
    return pltpu.with_memory_space_constraint(array, pltpu.HBM)


def flip_right(rp, rp32, rpt):
    W, D, _ = rp.shape
    rp32[...] = rp[...].reshape(W * D, W).astype(F32)
    for t in range(D):
        rpt[t // 2, :, (t % 2) * W : (t % 2 + 1) * W] = rp32[pl.ds(t, W, stride=D), :].astype(BF16)


def contract_right(x, rpt, h):
    n, D, W = x.shape
    rows = x[...].reshape(n * D, W)
    for t in range(0, D, 2):
        y = jnp.dot(rows, rpt[t // 2], preferred_element_type=F32).astype(BF16)
        h[t] = y[:, :W].reshape(n, D, W)
        h[t + 1] = y[:, W:].reshape(n, D, W)


def contract_layer(r, h, w, at=0, n=None, unroll=32):
    D, W = h.shape[0], h.shape[-1]
    n = h.shape[1] if n is None else n
    layer = r[...]

    def step(i, _):
        a = at + 2 * i
        pair = [h[:, a + k].reshape(D * D, W) for k in range(2)]
        y = jnp.dot(layer, jnp.concatenate(pair, axis=1), preferred_element_type=F32).astype(BF16)
        for k in range(2):
            w[:, a + k] = y[:, k * W : (k + 1) * W].reshape(D, D, W)
        return 0

    lax.fori_loop(0, n // 2, step, 0, unroll=unroll)


def flip_left(lp, lpt):
    D, W = lp.shape[1:]
    lpt[...] = lp[:W].reshape(W * D, W).T


def live_mask(lp, keep_right):
    W = lp.shape[-1]
    keep_left = lp[W, 0:1, :].astype(F32)
    rows = lax.broadcasted_iota(jnp.int32, (W, W), 0).astype(F32)
    lanes = lax.broadcasted_iota(jnp.int32, (W, W), 1)
    return (rows < keep_left) & (lanes < keep_right)


def contract_left(lpt, w, acc, at=0, n=None, carried=None, live=None):
    D, W = w.shape[0], w.shape[-1]
    n = w.shape[1] if n is None else n
    left = lpt[:, at * D : (at + n) * D]
    for q in range(0, D, 2):
        pair = [w[q + k, at : at + n].reshape(n * D, W) for k in range(2)]
        y = jnp.dot(left, jnp.concatenate(pair, axis=1), preferred_element_type=F32)
        for k in range(2):
            rows = pl.ds(q + k, W, stride=D)
            z = y[:, k * W : (k + 1) * W]
            if carried is not None:
                z = z + carried[rows, :]
            if live is not None:
                z = jnp.where(live, z, 0.0)
            acc[rows, :] = z


def store(acc, outs):
    at = 0
    for out in outs:
        n, D, W = out.shape
        out[...] = acc[at * D : (at + n) * D, :].astype(BF16).reshape(out.shape)
        at += n


def spread_layer(raw, r32, r):
    D = raw.shape[0]
    rows = lax.broadcasted_iota(jnp.int32, (D, D * D), 0)
    lanes = lax.broadcasted_iota(jnp.int32, (D, D * D), 1)
    total = jnp.zeros((D * D, D * D), F32)
    for p in range(D):
        place = (lanes == rows * D + p).astype(BF16)
        total += jnp.dot(raw[:, p].reshape(D * D, D), place, preferred_element_type=F32)
    n, W = D * D, r32.shape[1]
    for i in range(n // W):
        r32[i * n : (i + 1) * n, :] = total[:, i * W : (i + 1) * W]
        for q in range(D):
            r[q * D : (q + 1) * D, i * W : (i + 1) * W] = r32[pl.ds(i * n + q, D, stride=D), :].astype(BF16)


def load(src, dst, sem):
    copy = pltpu.make_async_copy(src, dst, sem)
    copy.start()
    return copy


def send_block(s, left_proj, out, sem):
    return load(left_proj.at[0, 0, s], out.at[pl.ds(0, left_proj.shape[3])], sem)


def add_kept(kept, s, out):
    out[out.shape[0] - 1] = jnp.full(out.shape[1:], kept[0, 0, s].astype(F32), F32).astype(BF16)


def first_kernel(kept_in, left_proj, out, kept, sems):
    counts = load(kept_in, kept, sems.at[1])
    copy = send_block(0, left_proj, out, sems.at[0])
    counts.wait()
    add_kept(kept, 0, out)
    copy.wait()


def head_kernel(band, kept, boundary, right, row_tensor, left_proj, first, wide, r, left, x, rp, raw, r32, rp32, rpt, h, sems):
    layer = load(row_tensor.at[0, 0], raw, sems.at[0])
    copy = send_block(1, left_proj, left, sems.at[1])
    add_kept(kept, 1, left)

    @pl.when(band[0] == 0)
    def _():
        a = load(right.at[0, 0, 0], rp, sems.at[2])
        b = load(boundary.at[0, 0], x, sems.at[3])
        a.wait()
        flip_right(rp, rp32, rpt)
        b.wait()
        contract_right(x, rpt, h)

    layer.wait()
    spread_layer(raw, r32, r)

    @pl.when(band[0] == 0)
    def _():
        contract_layer(r, h, wide)

    copy.wait()


def wide_kernel(s, n_before, prepares, band, *refs):
    refs = list(refs[n_before:])
    boundary, right, r, wide = (refs.pop(0) for _ in range(4))
    ahead = refs.pop(0) if prepares else None
    rp32, rpt, h = refs

    @pl.when(band[0] == 0)
    def _():
        flip_right(right.at[0, 0, s], rp32, rpt)
        contract_right(boundary.at[0, s], rpt, h)
        contract_layer(r, h, wide, unroll=8)

    if prepares:

        @pl.when(band[0] == 1)
        def _():
            for k in range(right.shape[2]):
                flip_right(right.at[0, 0, k], rp32, ahead.at[k])


def tail_kernel(s, n_out, sends, band, kept, left, wide, *refs):
    refs = list(refs)
    left_proj = refs.pop(0) if sends else None
    outs = [refs.pop(0) for _ in range(n_out)]
    lpt = refs.pop(0)
    send = refs.pop(0) if sends else None
    acc, sems = refs
    if sends:
        copy = send_block(s + 2, left_proj, send, sems.at[0])
        add_kept(kept, s + 2, send)
    flip_left(left, lpt)

    @pl.when(band[0] == 0)
    def _():
        contract_left(lpt, wide, acc, live=live_mask(left, kept[0, 0, s]))
        store(acc, outs)

    if sends:
        copy.wait()


def lower_kernel(s, part, parts, carried, n_before, band, kept, *refs):
    refs = list(refs[n_before:])
    before = refs.pop(0) if carried else None
    arrived, rpt, r, left, lpt, out, h, w, acc = refs
    n = arrived.shape[0]
    last = part == parts - 1

    @pl.when(band[0] == 1)
    def _():
        contract_right(arrived, rpt.at[s], h)
        contract_layer(r, h, w)
        half = lpt.at[:, pl.ds(part * n * h.shape[0], n * h.shape[0])]
        live = live_mask(left, kept[0, 0, s]) if last else None
        contract_left(half, w, acc if last else out, carried=before, live=live)
        if last:
            store(acc, [out])


def end_kernel(s, part, own_places, band, kept, *refs):
    refs = list(refs)
    own = [refs.pop(0) for _ in own_places]
    done = [refs.pop(0) for _ in range(s)]
    before, arrived, rpt, r, left, lpt, out, h, w, acc, block, sems = refs
    n, D, W = arrived.shape

    @pl.when(band[0] == 0)
    def _():
        copies = [
            load(piece, out.at[0, 0, k, pl.ds(at, piece.shape[0])], sems.at[i])
            for i, (piece, (k, at)) in enumerate(zip(own, own_places))
        ]
        for copy in copies:
            copy.wait()

    @pl.when(band[0] == 1)
    def _():
        copies = [load(piece, out.at[0, 0, k], sems.at[k]) for k, piece in enumerate(done)]
        contract_right(arrived, rpt.at[s], h)
        contract_layer(r, h, w)
        half = lpt.at[:, pl.ds(part * n * D, n * D)]
        contract_left(half, w, acc, carried=before, live=live_mask(left, kept[0, 0, s]))
        step = block.shape[0] // 4
        for i in range(4):
            rows = pl.ds(i * step, step)
            block[rows] = acc[i * step * D : (i + 1) * step * D, :].astype(BF16).reshape(step, D, W)
            copies.append(load(block.at[rows], out.at[0, 0, s, rows], sems.at[s + i]))
        for copy in copies:
            copy.wait()


def body(boundary, row_tensor, right_proj, left_proj, kept):
    _, sectors, W, D, _ = boundary.shape
    band = lax.axis_index("band").astype(jnp.int32)[None]
    down = [(0, 1)]
    splits = [2] + [1] * (sectors - 2) + [2]

    block = pltpu.VMEM((W, D, W), BF16)
    ext = pltpu.VMEM((W + 1, D, W), BF16)
    layer = pltpu.VMEM((D * D, D * D), BF16)
    wide_shape = pltpu.VMEM((D, W, D, W), BF16)
    rp32, lpt, acc = pltpu.VMEM((W * D, W), F32), pltpu.VMEM((W, W * D), BF16), pltpu.VMEM((W * D, W), F32)

    def wide_part(n):
        return pltpu.VMEM((D, n, D, W), BF16)

    def cost(part):
        return pl.CostEstimate(
            flops=int(8 * part * W * D * W * W * D), bytes_accessed=8 * W * D * W, transcendentals=0
        )

    def call(kernel, name, part, in_specs, outs, scratch, **kw):
        single = len(outs) == 1
        specs = [ANY if isinstance(o, jax.ShapeDtypeStruct) else VMEM for o in outs]
        return pl.pallas_call(
            kernel, out_shape=outs[0] if single else outs, in_specs=in_specs,
            out_specs=specs[0] if single else specs, scratch_shapes=scratch,
            compiler_params=PARAMS, cost_estimate=cost(part), name=name, **kw,
        )

    rpt = pltpu.VMEM((D // 2, W, 2 * W), BF16)
    dma = pltpu.SemaphoreType.DMA((sectors + 4,))
    direct, (hop, rest) = straight(), around()
    axes = ("col", "band")
    first = call(first_kernel, "first", 0.1, [HBM, HBM], [ext], [pltpu.SMEM(kept.shape, jnp.int32), dma])(
        in_hbm(kept), in_hbm(left_proj)
    )
    left = [in_vmem(lax.ppermute(first, axes, direct))]
    wide, r, send = call(
        head_kernel, "head", 0.75, [SMEM, SMEM] + [HBM] * 4 + [ANY], [wide_shape, layer, ext],
        [block, block, pltpu.VMEM((D, D, D, D), BF16), pltpu.VMEM((D * D * D * D // W, W), F32), rp32, rpt, wide_shape, dma],
    )(band, kept, in_hbm(boundary), in_hbm(right_proj), in_hbm(row_tensor), in_hbm(left_proj), first)
    r, near, right = in_vmem(r), in_vmem(boundary), in_vmem(right_proj)
    states, arrived, flipped = [], [], []

    def tail(s, wide, sends=False):
        k, extra = splits[s], [in_hbm(left_proj)] if sends else []
        outs = call(
            functools.partial(tail_kernel, s, k, sends), "tail", 0.25, [SMEM, SMEM, VMEM, VMEM] + [HBM] * len(extra),
            [pltpu.VMEM((W // k, D, W), BF16)] * k + [lpt] + [ext] * len(extra), [acc, dma],
        )(band, kept, left[s], in_vmem(wide), *extra)
        states.append(list(outs[:k]))
        flipped.append(in_vmem(outs[k]))
        arrived.append([])
        return outs[k + 1 :]

    def give(s, part=0):
        arrived[s].append(lax.ppermute(states[s][part], "band", down))

    def widen(s, before, prepares=False):
        return call(
            functools.partial(wide_kernel, s, len(before), prepares), "wide", 0.75,
            [SMEM] + [ANY] * len(before) + [VMEM] * 3,
            [wide_shape] + ([pltpu.VMEM((sectors, *rpt.shape), BF16)] if prepares else []), [rp32, rpt, wide_shape],
        )(band, *before, near, right, r)

    def lower(s, part, before, total=None):
        k = splits[s]
        carried = [] if total is None else [in_vmem(total)]
        operands = carried + [in_vmem(arrived[s][part]), ahead, r, left[s], flipped[s]]
        return call(
            functools.partial(lower_kernel, s, part, k, bool(carried), len(before)), "lower", 1 / k,
            [SMEM, SMEM] + [ANY] * len(before) + [VMEM] * len(operands), [block if part == k - 1 else acc],
            [wide_part(W // k), wide_part(W // k), acc],
        )(band, kept, *before, *operands)

    left.append(in_vmem(lax.ppermute(send, axes, direct)))
    (send,) = tail(0, wide, True)
    give(0)
    part_way = lax.ppermute(send, axes, hop)
    wide, ahead = widen(1, [states[0][0]], True)
    states[0][1], wide = lax.optimization_barrier((states[0][1], wide))
    give(0, 1)
    ahead = in_vmem(ahead)
    tail(1, wide)
    give(1)
    part_way, states[1][0] = lax.optimization_barrier((part_way, states[1][0]))
    left.append(in_vmem(lax.ppermute(part_way, axes, rest)))
    wide = widen(2, [part_way])
    done = [lower(0, 1, [], lower(0, 0, [wide]))]
    tail(2, wide)
    give(2)
    give(2, 1)
    done.append(lower(1, 0, [states[2][0], done[0]]))
    s, k = sectors - 1, splits[-1]
    total = lower(s, 0, [done[1]])
    own = [x for state in states for x in state]
    places = [(i, W // splits[i] * j) for i in range(sectors) for j in range(splits[i])]
    operands = own + done + [total, arrived[s][k - 1]]
    return call(
        functools.partial(end_kernel, s, k - 1, places), "end", 1 / k, [SMEM, SMEM] + [VMEM] * (len(operands) + 4),
        [jax.ShapeDtypeStruct((1, 1, sectors, W, D, W), BF16)],
        [wide_part(W // k), wide_part(W // k), acc, block, dma],
    )(band, kept, *[in_vmem(x) for x in operands], ahead, r, left[s], flipped[s])


def solution(mesh):
    in_specs = (
        P("col", None, None, None, None),
        P("band", "col", None, None, None, None),
        P("band", "col", None, None, None, None),
        P("band", "col", None, None, None, None),
        P("band", "col", None),
    )
    out_specs = P("band", "col", None, None, None, None)
    return jax.shard_map(body, mesh=mesh, in_specs=in_specs, out_specs=out_specs, check_vma=False)
```

```python
import functools

import jax
import jax.numpy as jnp
from jax import lax
from jax.experimental import pallas as pl
from jax.experimental.pallas import tpu as pltpu
from jax.sharding import PartitionSpec as P

F32, BF16 = jnp.float32, jnp.bfloat16
ANY = pl.BlockSpec(memory_space=pl.ANY)
HBM = pl.BlockSpec(memory_space=pltpu.HBM)
SMEM = pl.BlockSpec(memory_space=pltpu.SMEM)
VMEM = pl.BlockSpec(memory_space=pltpu.VMEM)
PARAMS = pltpu.CompilerParams(vmem_limit_bytes=28 << 20)


X, Y_HI, Z, CORES, BANDS = 4, 2, 8, 2, 2
COLS = X * Y_HI * Z * CORES


def place(column, band):
    return column * BANDS + band


def straight():
    return [(place((c - 1) % COLS, b), place(c, b)) for c in range(COLS) for b in range(BANDS)]


def around():
    first, second = [], []
    for c in range(COLS):
        for b in range(BANDS):
            here, there = place(c, b), place((c + 1) % COLS, b)
            if (c + 1) % (Z * CORES):
                first.append((here, there))
                second.append((there, there))
            else:
                x, y_hi = divmod(c // (Z * CORES), Y_HI)
                y = (y_hi * BANDS + b - 1) % (Y_HI * BANDS)
                via = place((x * Y_HI + y // BANDS) * Z * CORES, y % BANDS)
                first.append((here, via))
                second.append((via, there))
    return first, second


def in_vmem(array):
    return pltpu.with_memory_space_constraint(array, pltpu.VMEM)


def in_hbm(array):
    return pltpu.with_memory_space_constraint(array, pltpu.HBM)


def flip_right(rp, rp32, rpt):
    W, D, _ = rp.shape
    rp32[...] = rp[...].reshape(W * D, W).astype(F32)
    for t in range(D):
        rpt[t // 2, :, (t % 2) * W : (t % 2 + 1) * W] = rp32[pl.ds(t, W, stride=D), :].astype(BF16)


def contract_right(x, rpt, h):
    n, D, W = x.shape
    rows = x[...].reshape(n * D, W)
    for t in range(0, D, 2):
        y = jnp.dot(rows, rpt[t // 2], preferred_element_type=F32).astype(BF16)
        h[t] = y[:, :W].reshape(n, D, W)
        h[t + 1] = y[:, W:].reshape(n, D, W)


def contract_layer(r, h, w, at=0, n=None, unroll=32):
    D, W = h.shape[0], h.shape[-1]
    n = h.shape[1] if n is None else n
    layer = r[...]

    def step(i, _):
        a = at + 2 * i
        pair = [h[:, a + k].reshape(D * D, W) for k in range(2)]
        y = jnp.dot(layer, jnp.concatenate(pair, axis=1), preferred_element_type=F32).astype(BF16)
        for k in range(2):
            w[:, a + k] = y[:, k * W : (k + 1) * W].reshape(D, D, W)
        return 0

    lax.fori_loop(0, n // 2, step, 0, unroll=unroll)


def flip_left(lp, lpt):
    D, W = lp.shape[1:]
    lpt[...] = lp[:W].reshape(W * D, W).T


def live_mask(lp, keep_right):
    W = lp.shape[-1]
    keep_left = lp[W, 0:1, :].astype(F32)
    rows = lax.broadcasted_iota(jnp.int32, (W, W), 0).astype(F32)
    lanes = lax.broadcasted_iota(jnp.int32, (W, W), 1)
    return (rows < keep_left) & (lanes < keep_right)


def contract_left(lpt, w, acc, at=0, n=None, carried=None, live=None):
    D, W = w.shape[0], w.shape[-1]
    n = w.shape[1] if n is None else n
    left = lpt[:, at * D : (at + n) * D]
    for q in range(0, D, 2):
        pair = [w[q + k, at : at + n].reshape(n * D, W) for k in range(2)]
        y = jnp.dot(left, jnp.concatenate(pair, axis=1), preferred_element_type=F32)
        for k in range(2):
            rows = pl.ds(q + k, W, stride=D)
            z = y[:, k * W : (k + 1) * W]
            if carried is not None:
                z = z + carried[rows, :]
            if live is not None:
                z = jnp.where(live, z, 0.0)
            acc[rows, :] = z


def store(acc, outs):
    at = 0
    for out in outs:
        n, D, W = out.shape
        out[...] = acc[at * D : (at + n) * D, :].astype(BF16).reshape(out.shape)
        at += n


def spread_layer(raw, r32, r):
    D = raw.shape[0]
    rows = lax.broadcasted_iota(jnp.int32, (D, D * D), 0)
    lanes = lax.broadcasted_iota(jnp.int32, (D, D * D), 1)
    total = jnp.zeros((D * D, D * D), F32)
    for p in range(D):
        place = (lanes == rows * D + p).astype(BF16)
        total += jnp.dot(raw[:, p].reshape(D * D, D), place, preferred_element_type=F32)
    n, W = D * D, r32.shape[1]
    for i in range(n // W):
        r32[i * n : (i + 1) * n, :] = total[:, i * W : (i + 1) * W]
        for q in range(D):
            r[q * D : (q + 1) * D, i * W : (i + 1) * W] = r32[pl.ds(i * n + q, D, stride=D), :].astype(BF16)


def load(src, dst, sem):
    copy = pltpu.make_async_copy(src, dst, sem)
    copy.start()
    return copy


def send_block(s, left_proj, out, sem):
    return load(left_proj.at[0, 0, s], out.at[pl.ds(0, left_proj.shape[3])], sem)


def add_kept(kept, s, out):
    out[out.shape[0] - 1] = jnp.full(out.shape[1:], kept[0, 0, s].astype(F32), F32).astype(BF16)


def first_kernel(kept_in, left_proj, out, kept, sems):
    counts = load(kept_in, kept, sems.at[1])
    copy = send_block(0, left_proj, out, sems.at[0])
    counts.wait()
    add_kept(kept, 0, out)
    copy.wait()


def head_kernel(band, kept, boundary, right, row_tensor, left_proj, first, wide, r, left, later, x, rp, raw, r32, rp32, rpt, h, sems):
    layer = load(row_tensor.at[0, 0], raw, sems.at[0])
    copies = [send_block(1, left_proj, left, sems.at[1]), send_block(2, left_proj, later, sems.at[4])]
    add_kept(kept, 1, left)
    add_kept(kept, 2, later)

    @pl.when(band[0] == 0)
    def _():
        a = load(right.at[0, 0, 0], rp, sems.at[2])
        b = load(boundary.at[0, 0], x, sems.at[3])
        a.wait()
        flip_right(rp, rp32, rpt)
        b.wait()
        contract_right(x, rpt, h)

    layer.wait()
    spread_layer(raw, r32, r)

    @pl.when(band[0] == 0)
    def _():
        contract_layer(r, h, wide)

    for copy in copies:
        copy.wait()


def wide_kernel(s, n_before, prepares, band, *refs):
    refs = list(refs[n_before:])
    boundary, right, r, wide = (refs.pop(0) for _ in range(4))
    ahead = refs.pop(0) if prepares else None
    rp32, rpt, h = refs

    @pl.when(band[0] == 0)
    def _():
        flip_right(right.at[0, 0, s], rp32, rpt)
        contract_right(boundary.at[0, s], rpt, h)
        contract_layer(r, h, wide, unroll=8)

    if prepares:

        @pl.when(band[0] == 1)
        def _():
            for k in range(right.shape[2]):
                flip_right(right.at[0, 0, k], rp32, ahead.at[k])


def tail_kernel(s, n_out, sends, band, kept, left, wide, *refs):
    refs = list(refs)
    left_proj = refs.pop(0) if sends else None
    outs = [refs.pop(0) for _ in range(n_out)]
    lpt = refs.pop(0)
    send = refs.pop(0) if sends else None
    acc, sems = refs
    if sends:
        copy = send_block(s + 2, left_proj, send, sems.at[0])
        add_kept(kept, s + 2, send)
    flip_left(left, lpt)

    @pl.when(band[0] == 0)
    def _():
        contract_left(lpt, wide, acc, live=live_mask(left, kept[0, 0, s]))
        store(acc, outs)

    if sends:
        copy.wait()


def lower_kernel(s, part, parts, carried, n_before, band, kept, *refs):
    refs = list(refs[n_before:])
    before = refs.pop(0) if carried else None
    arrived, rpt, r, left, lpt, out, h, w, acc = refs
    n = arrived.shape[0]
    last = part == parts - 1

    @pl.when(band[0] == 1)
    def _():
        contract_right(arrived, rpt.at[s], h)
        contract_layer(r, h, w)
        half = lpt.at[:, pl.ds(part * n * h.shape[0], n * h.shape[0])]
        live = live_mask(left, kept[0, 0, s]) if last else None
        contract_left(half, w, acc if last else out, carried=before, live=live)
        if last:
            store(acc, [out])


def end_kernel(s, part, own_places, band, kept, *refs):
    refs = list(refs)
    own = [refs.pop(0) for _ in own_places]
    done = [refs.pop(0) for _ in range(s)]
    before, arrived, rpt, r, left, lpt, out, h, w, acc, block, sems = refs
    n, D, W = arrived.shape

    @pl.when(band[0] == 0)
    def _():
        copies = [
            load(piece, out.at[0, 0, k, pl.ds(at, piece.shape[0])], sems.at[i])
            for i, (piece, (k, at)) in enumerate(zip(own, own_places))
        ]
        for copy in copies:
            copy.wait()

    @pl.when(band[0] == 1)
    def _():
        copies = [load(piece, out.at[0, 0, k], sems.at[k]) for k, piece in enumerate(done)]
        contract_right(arrived, rpt.at[s], h)
        contract_layer(r, h, w)
        half = lpt.at[:, pl.ds(part * n * D, n * D)]
        contract_left(half, w, acc, carried=before, live=live_mask(left, kept[0, 0, s]))
        step = block.shape[0] // 4
        for i in range(4):
            rows = pl.ds(i * step, step)
            block[rows] = acc[i * step * D : (i + 1) * step * D, :].astype(BF16).reshape(step, D, W)
            copies.append(load(block.at[rows], out.at[0, 0, s, rows], sems.at[s + i]))
        for copy in copies:
            copy.wait()


def body(boundary, row_tensor, right_proj, left_proj, kept):
    _, sectors, W, D, _ = boundary.shape
    band = lax.axis_index("band").astype(jnp.int32)[None]
    down = [(0, 1)]
    splits = [2] + [1] * (sectors - 2) + [2]

    block = pltpu.VMEM((W, D, W), BF16)
    ext = pltpu.VMEM((W + 1, D, W), BF16)
    layer = pltpu.VMEM((D * D, D * D), BF16)
    wide_shape = pltpu.VMEM((D, W, D, W), BF16)
    rp32, lpt, acc = pltpu.VMEM((W * D, W), F32), pltpu.VMEM((W, W * D), BF16), pltpu.VMEM((W * D, W), F32)

    def wide_part(n):
        return pltpu.VMEM((D, n, D, W), BF16)

    def cost(part):
        return pl.CostEstimate(
            flops=int(8 * part * W * D * W * W * D), bytes_accessed=8 * W * D * W, transcendentals=0
        )

    def call(kernel, name, part, in_specs, outs, scratch, **kw):
        single = len(outs) == 1
        specs = [ANY if isinstance(o, jax.ShapeDtypeStruct) else VMEM for o in outs]
        return pl.pallas_call(
            kernel, out_shape=outs[0] if single else outs, in_specs=in_specs,
            out_specs=specs[0] if single else specs, scratch_shapes=scratch,
            compiler_params=PARAMS, cost_estimate=cost(part), name=name, **kw,
        )

    rpt = pltpu.VMEM((D // 2, W, 2 * W), BF16)
    dma = pltpu.SemaphoreType.DMA((sectors + 4,))
    direct, (hop, rest) = straight(), around()
    axes = ("col", "band")
    first = call(first_kernel, "first", 0.1, [HBM, HBM], [ext], [pltpu.SMEM(kept.shape, jnp.int32), dma])(
        in_hbm(kept), in_hbm(left_proj)
    )
    left = [in_vmem(lax.ppermute(first, axes, direct))]
    wide, r, send, later = call(
        head_kernel, "head", 0.75, [SMEM, SMEM] + [HBM] * 4 + [ANY], [wide_shape, layer, ext, ext],
        [block, block, pltpu.VMEM((D, D, D, D), BF16), pltpu.VMEM((D * D * D * D // W, W), F32), rp32, rpt, wide_shape, dma],
    )(band, kept, in_hbm(boundary), in_hbm(right_proj), in_hbm(row_tensor), in_hbm(left_proj), first)
    r, near, right = in_vmem(r), in_vmem(boundary), in_vmem(right_proj)
    states, arrived, flipped = [], [], []

    def tail(s, wide, sends=False):
        k, extra = splits[s], [in_hbm(left_proj)] if sends else []
        outs = call(
            functools.partial(tail_kernel, s, k, sends), "tail", 0.25, [SMEM, SMEM, VMEM, VMEM] + [HBM] * len(extra),
            [pltpu.VMEM((W // k, D, W), BF16)] * k + [lpt] + [ext] * len(extra), [acc, dma],
        )(band, kept, left[s], in_vmem(wide), *extra)
        states.append(list(outs[:k]))
        flipped.append(in_vmem(outs[k]))
        arrived.append([])
        return outs[k + 1 :]

    def give(s, part=0):
        arrived[s].append(lax.ppermute(states[s][part], "band", down))

    def widen(s, before, prepares=False):
        return call(
            functools.partial(wide_kernel, s, len(before), prepares), "wide", 0.75,
            [SMEM] + [ANY] * len(before) + [VMEM] * 3,
            [wide_shape] + ([pltpu.VMEM((sectors, *rpt.shape), BF16)] if prepares else []), [rp32, rpt, wide_shape],
        )(band, *before, near, right, r)

    def lower(s, part, before, total=None):
        k = splits[s]
        carried = [] if total is None else [in_vmem(total)]
        operands = carried + [in_vmem(arrived[s][part]), ahead, r, left[s], flipped[s]]
        return call(
            functools.partial(lower_kernel, s, part, k, bool(carried), len(before)), "lower", 1 / k,
            [SMEM, SMEM] + [ANY] * len(before) + [VMEM] * len(operands), [block if part == k - 1 else acc],
            [wide_part(W // k), wide_part(W // k), acc],
        )(band, kept, *before, *operands)

    left.append(in_vmem(lax.ppermute(send, axes, direct)))
    tail(0, wide)
    later, states[0][0] = lax.optimization_barrier((later, states[0][0]))
    give(0)
    part_way = lax.ppermute(later, axes, hop)
    wide, ahead = widen(1, [states[0][0]], True)
    states[0][1], wide = lax.optimization_barrier((states[0][1], wide))
    give(0, 1)
    ahead = in_vmem(ahead)
    tail(1, wide)
    give(1)
    part_way, states[1][0] = lax.optimization_barrier((part_way, states[1][0]))
    left.append(in_vmem(lax.ppermute(part_way, axes, rest)))
    wide = widen(2, [part_way])
    done = [lower(0, 1, [], lower(0, 0, [wide]))]
    tail(2, wide)
    give(2)
    give(2, 1)
    done.append(lower(1, 0, [states[2][0], done[0]]))
    s, k = sectors - 1, splits[-1]
    total = lower(s, 0, [done[1]])
    own = [x for state in states for x in state]
    places = [(i, W // splits[i] * j) for i in range(sectors) for j in range(splits[i])]
    operands = own + done + [total, arrived[s][k - 1]]
    return call(
        functools.partial(end_kernel, s, k - 1, places), "end", 1 / k, [SMEM, SMEM] + [VMEM] * (len(operands) + 4),
        [jax.ShapeDtypeStruct((1, 1, sectors, W, D, W), BF16)],
        [wide_part(W // k), wide_part(W // k), acc, block, dma],
    )(band, kept, *[in_vmem(x) for x in operands], ahead, r, left[s], flipped[s])


def solution(mesh):
    in_specs = (
        P("col", None, None, None, None),
        P("band", "col", None, None, None, None),
        P("band", "col", None, None, None, None),
        P("band", "col", None, None, None, None),
        P("band", "col", None),
    )
    out_specs = P("band", "col", None, None, None, None)
    return jax.shard_map(body, mesh=mesh, in_specs=in_specs, out_specs=out_specs, check_vma=False)
```
